128 devices in a mesh: row: 8 (over x, y_lo), col: 16 (over z, y_hi, core).
Axes of the slice: x: 4, y: 4 (y_hi: 2, y_lo: 2; y = y_hi * 2 + y_lo), z: 4, core: 2. Of those that a mesh axis runs over, the one named last changes fastest.
Arguments:
- alignment_left: bfloat16 [1024, 16384], P(('row', 'col')), may hold values from -6 to 6
- alignment_right: bfloat16 [512, 32768], P('row', 'col'), may hold values from -6 to 6
- pair_features: bfloat16 [1024, 1024, 128], P('row', 'col'), may hold values from -6 to 6
- output_weight: bfloat16 [1024, 128], replicated, may hold values from -4 to 4
- output_bias: float32 [128], replicated, may hold values from -4 to 4
- norm_scale_gain: float32 [128], replicated, may hold values from 0.1 to 1.9
- projection_weight: bfloat16 [128, 512], replicated, may hold values from -0.5 to 0.5
- gate_offset_bias: float32 [128], replicated, may hold values from -4 to 4
Outputs:
- new_pair: bfloat16 [1024, 1024, 128], P('row', 'col')
- projections: bfloat16 [1024, 512, 1024], P('row', 'col')
The draws below stay inside these ranges and needn't reach their ends.
All inputs are finite; a program needn't handle non-finite values.
Results may differ from the reference program's by a relative error of at most 0.0058.
Values may be sent and summed in bfloat16 or wider, within the bound.
A program may use at most 192 MiB of HBM per device.

```python
import jax
import jax.numpy as jnp
from jax import lax

CHANNEL_WIDTH = 32
CZ = 128
HEADS = 4
DH = 32
ALIGNMENT_ROWS = 512
RESIDUE_COUNT = 1024
PROJ = 512


def levels(rng, extent, split, low, largest):
    gain, own = 1.0, jax.random.fold_in(rng, 6)
    for dim, parts in split:
        steps = jnp.exp(jax.random.uniform(jax.random.fold_in(own, dim), (parts,), jnp.float32, low / len(split), largest / len(split)))
        gain = gain * jnp.repeat(steps, extent[dim] // parts).reshape([-1 if axis == dim else 1 for axis in range(len(extent))])
    return gain


def noise(rng, extent, scale, limit, pieces=(), dtype=jnp.bfloat16):
    result = scale * jax.random.normal(rng, extent, jnp.float32)
    if pieces:
        result = result * levels(rng, extent, pieces, -0.22, 0.18)
    return jnp.clip(result, -limit, limit).astype(dtype)


def setup_inputs(seed: int = 0) -> dict:
    splits = jax.random.split(jax.random.key(seed), 9)
    alignment_left = noise(splits[0], (RESIDUE_COUNT, CHANNEL_WIDTH * ALIGNMENT_ROWS), 1.0, 6.0, ((0, 128),))
    alignment_right = noise(splits[1], (ALIGNMENT_ROWS, RESIDUE_COUNT * CHANNEL_WIDTH), 1.0, 6.0, ((0, 8), (1, 16)))
    pair_features = noise(splits[2], (RESIDUE_COUNT, RESIDUE_COUNT, CZ), 1.0, 6.0, ((0, 8), (1, 16)))
    output_weight = noise(splits[3], (CHANNEL_WIDTH * CHANNEL_WIDTH, CZ), (CHANNEL_WIDTH * CHANNEL_WIDTH // ALIGNMENT_ROWS) ** -0.5, 4.0)
    output_bias = noise(splits[4], (CZ,), 1.0, 4.0, (), jnp.float32)
    norm_scale_gain = jnp.clip(1.0 + 0.18 * jax.random.normal(splits[5], (CZ,), jnp.float32), 0.1, 1.9)
    projection_weight = noise(splits[6], (CZ, PROJ), CZ ** -0.5, 0.5)
    gate_offset_bias = noise(splits[7], (HEADS * DH,), 1.0, 4.0, (), jnp.float32)
    return {"alignment_left": alignment_left, "alignment_right": alignment_right, "pair_features": pair_features, "output_weight": output_weight, "output_bias": output_bias, "norm_scale_gain": norm_scale_gain, "projection_weight": projection_weight, "gate_offset_bias": gate_offset_bias}


norm_eps = 1e-05

def project(values, norm_scale_gain, projection_weight, gate_offset_bias):
    widened = values.astype(jnp.float32)
    average = lax.optimization_barrier(jnp.mean(widened, axis=-1, keepdims=True))
    centred = widened - average
    variance = lax.optimization_barrier(jnp.mean(centred * centred, axis=-1, keepdims=True))
    normed = (centred * lax.rsqrt(variance + norm_eps) * norm_scale_gain).astype(jnp.bfloat16)
    projected = jnp.dot(normed, projection_weight, preferred_element_type=jnp.float32)
    quarter = projection_weight.shape[1] // 4
    head_part = projected[..., :3 * quarter]
    gate_part = jax.nn.sigmoid(projected[..., 3 * quarter:] + gate_offset_bias)
    return jnp.concatenate([head_part, gate_part], axis=-1).astype(jnp.bfloat16)

def reference(alignment_left, alignment_right, pair_features, output_weight, output_bias, norm_scale_gain, projection_weight, gate_offset_bias):
    block_length = 64
    total_blocks = RESIDUE_COUNT // block_length
    left_residue_blocks = alignment_left.reshape(total_blocks, block_length, CHANNEL_WIDTH, ALIGNMENT_ROWS)
    pair_blocks = pair_features.reshape(total_blocks, block_length, RESIDUE_COUNT, CZ)

    def one_block(inputs):
        left_residue_block, pair_block = inputs
        channel_products = lax.dot_general(left_residue_block, alignment_right, (((2,), (0,)), ((), ())), preferred_element_type=jnp.float32)
        outer_product_average = (channel_products / ALIGNMENT_ROWS).astype(jnp.bfloat16)
        outer_product_average = outer_product_average.reshape(block_length, CHANNEL_WIDTH, RESIDUE_COUNT, CHANNEL_WIDTH).transpose(0, 2, 1, 3).reshape(block_length * RESIDUE_COUNT, CHANNEL_WIDTH * CHANNEL_WIDTH)
        update = jnp.dot(outer_product_average, output_weight, preferred_element_type=jnp.float32) + output_bias
        fresh = (pair_block.astype(jnp.float32).reshape(block_length * RESIDUE_COUNT, CZ) + update).astype(jnp.bfloat16)
        projected = project(fresh, norm_scale_gain, projection_weight, gate_offset_bias)
        return (fresh.reshape(block_length, RESIDUE_COUNT, CZ), projected.reshape(block_length, RESIDUE_COUNT, PROJ))
    new_blocks, proj_blocks = lax.map(one_block, (left_residue_blocks, pair_blocks))
    new_pair = new_blocks.reshape(RESIDUE_COUNT, RESIDUE_COUNT, CZ)
    projections = jnp.transpose(proj_blocks.reshape(RESIDUE_COUNT, RESIDUE_COUNT, PROJ), (1, 2, 0))
    return (new_pair, projections)
```

```python
import functools

import jax
import jax.numpy as jnp
from jax import lax
from jax.experimental import pallas as pl
from jax.experimental.pallas import tpu as pltpu
from jax.sharding import PartitionSpec as P

MESH = pl.DeviceIdType.MESH
bf16, f32 = jnp.bfloat16, jnp.float32
norm_eps = 1e-05

ROWS, COLS = 8, 16
TI, TJ, C, PROJ = 128, 64, 128, 512
W, S = 32, 512
GROUP = PROJ // COLS
JN = 4
NT = TJ // JN
LAG = 2


def kernel(
    left_hbm, right_hbm, pair_ref, weight_ref, bias_ref, gain_ref, proj_ref, gate_ref,
    new_ref, out,
    left, right, block_weight, proj_t, gate_t, outer, pair_f, new_f, send_buf, stage,
    load_sem, send1, recv1, send2, recv2,
):
    row, col = lax.axis_index("row"), lax.axis_index("col")
    y_lo = row % 2
    x2 = row - y_lo
    y_hi = (col // 2) % 2

    for c1 in range(W):
        pltpu.make_async_copy(left_hbm.at[:, pl.ds(c1 * S, S)], left.at[c1], load_sem.at[0]).start()
    for u in range(8):
        pltpu.make_async_copy(right_hbm.at[:, pl.ds(u * 256, 256)], right.at[u], load_sem.at[1]).start()

    block_weight[...] = jnp.zeros_like(block_weight)

    def fill(c1, _):
        w = weight_ref[pl.ds(pl.multiple_of(c1 * W, W), W), :]
        for j in range(4):
            block_weight[pl.ds(pl.multiple_of(c1 * 128 + j * W, W), W), j * C : (j + 1) * C] = w
        return 0

    lax.fori_loop(0, W, fill, 0)
    proj_t[...] = proj_ref[...].astype(f32).T.astype(bf16)
    gate_t[...] = jnp.broadcast_to(gate_ref[...], (C, C)).T

    pltpu.make_async_copy(left, left, load_sem.at[0]).wait()
    pltpu.make_async_copy(right, right, load_sem.at[1]).wait()

    def target(core, t, r):
        j0 = pl.multiple_of(core * TJ + t * JN, JN)
        return out.at[pl.ds(j0, JN), :, pl.ds(pl.multiple_of(r * TI, TI), TI)]

    def send(t):
        pltpu.make_async_copy(send_buf.at[t, col], stage.at[t, col], recv1.at[t, col]).start()

        def body(k, _):
            c2 = lax.bitwise_xor(col, k)
            r2 = x2 + (y_lo + y_hi + (c2 // 2) % 2) % 2
            pltpu.make_async_remote_copy(
                src_ref=send_buf.at[t, c2], dst_ref=stage.at[t, col], send_sem=send1, recv_sem=recv1.at[t, col],
                device_id=(r2, c2), device_id_type=MESH,
            ).start()
            return 0

        lax.fori_loop(1, COLS, body, 0)

    def forward(t):
        def piece(q, core, local):
            r2 = lax.bitwise_xor(row, q)
            origin = r2 * 2 + core
            r_origin = x2 + (y_lo + r2 % 2 + y_hi) % 2
            here = stage.at[t, origin]
            pltpu.make_async_copy(here, here, recv1.at[t, origin]).wait()
            if local:
                pltpu.make_async_copy(here, target(core, t, r_origin), recv2).start()
            else:
                pltpu.make_async_remote_copy(
                    src_ref=here, dst_ref=target(core, t, r_origin), send_sem=send2, recv_sem=recv2,
                    device_id=(r2, col), device_id_type=MESH,
                ).start()

        piece(0, 0, True)
        piece(0, 1, True)

        def body(m, _):
            piece(m // 2, m % 2, False)
            return 0

        lax.fori_loop(2, COLS, body, 0)

    def sixteen(v, _):
        j16 = pl.multiple_of(v * 16, 16)
        pair_f[...] = pair_ref[:, pl.ds(j16, 16), :].astype(f32).reshape(TI * 16, C)
        for half in range(2):
            u = v * 2 + half

            def products(b, _):
                lhs = left[pl.ds(b * 4, 4)].reshape(4 * TI, S)
                p = jnp.dot(lhs, right[u], preferred_element_type=f32)
                p = (p * (1.0 / S)).astype(bf16)
                for k in range(4):
                    for g in range(2):
                        outer[g * TI : (g + 1) * TI, pl.ds(pl.multiple_of(b * 512 + k * 128, 128), 128)] = p[
                            k * TI : (k + 1) * TI, g * 128 : (g + 1) * 128
                        ]
                return 0

            lax.fori_loop(0, W // 4, products, 0)
            update = jnp.dot(outer[...], block_weight[...], preferred_element_type=f32)
            for g in range(2):
                t = v * 4 + half * 2 + g
                for pairs in range(2):
                    both = []
                    for jj in range(2):
                        j = pairs * 2 + jj
                        j_in = half * 8 + g * 4 + j
                        add = update[g * TI : (g + 1) * TI, j * C : (j + 1) * C] + bias_ref[...]
                        fresh = (pair_f[pl.ds(j_in, TI, stride=16), :] + add).astype(bf16).astype(f32)
                        new_f[pl.ds(j_in, TI, stride=16), :] = fresh
                        average = jnp.mean(fresh, axis=-1, keepdims=True)
                        centred = fresh - average
                        variance = jnp.mean(centred * centred, axis=-1, keepdims=True)
                        both.append((centred * lax.rsqrt(variance + norm_eps) * gain_ref[...]).astype(bf16))
                    normed = jnp.concatenate(both, axis=0)
                    raw = lax.dot_general(
                        proj_t[...], normed, (((1,), (1,)), ((), ())), preferred_element_type=f32
                    )
                    for jj in range(2):
                        mine = raw[:, jj * TI : (jj + 1) * TI]
                        gate = jax.nn.sigmoid(mine[384:] + gate_t[...])
                        send_buf[t, 0:12, pairs * 2 + jj] = mine[:384].astype(bf16).reshape(12, GROUP, TI)
                        send_buf[t, 12:16, pairs * 2 + jj] = gate.astype(bf16).reshape(4, GROUP, TI)
                send(t)

                @pl.when(t >= LAG)
                def _():
                    forward(t - LAG)

        new_ref[:, pl.ds(j16, 16), :] = new_f[...].astype(bf16).reshape(TI, 16, C)
        return 0

    lax.fori_loop(0, TJ // 16, sixteen, 0)
    for t in range(NT - LAG, NT):
        forward(t)
    sent = send_buf.at[:, pl.ds(0, COLS - 1)]
    pltpu.make_async_copy(sent, sent, send1).wait()
    sent = stage.at[:, pl.ds(0, COLS - 2)]
    pltpu.make_async_copy(sent, sent, send2).wait()
    pltpu.make_async_copy(stage, stage, recv2).wait()


def shards(
    alignment_left, alignment_right, pair_features, output_weight, output_bias, norm_scale_gain, projection_weight,
    gate_offset_bias,
):
    right = lax.all_gather(alignment_right, "row", axis=0, tiled=True)
    left = lax.all_gather(alignment_left, "col", axis=0, tiled=True)
    vmem, anywhere = pl.BlockSpec(memory_space=pltpu.VMEM), pl.BlockSpec(memory_space=pl.ANY)
    return pl.pallas_call(
        kernel,
        out_shape=(
            jax.ShapeDtypeStruct((TI, TJ, C), bf16),
            jax.ShapeDtypeStruct((2 * TJ, GROUP, ROWS * TI), bf16),
        ),
        in_specs=[anywhere, anywhere] + [vmem] * 6,
        out_specs=(vmem, anywhere),
        scratch_shapes=[
            pltpu.VMEM((W, TI, S), bf16),
            pltpu.VMEM((8, S, 256), bf16),
            pltpu.VMEM((4 * W * W, 4 * C), bf16),
            pltpu.VMEM((PROJ, C), bf16),
            pltpu.VMEM((C, C), f32),
            pltpu.VMEM((2 * TI, W * 128), bf16),
            pltpu.VMEM((TI * 16, C), f32),
            pltpu.VMEM((TI * 16, C), f32),
            pltpu.VMEM((NT, COLS, JN, GROUP, TI), bf16),
            pltpu.VMEM((NT, COLS, JN, GROUP, TI), bf16),
            pltpu.SemaphoreType.DMA((2,)),
            pltpu.SemaphoreType.DMA,
            pltpu.SemaphoreType.DMA((NT, COLS)),
            pltpu.SemaphoreType.DMA,
            pltpu.SemaphoreType.DMA,
        ],
        compiler_params=pltpu.CompilerParams(has_side_effects=True, vmem_limit_bytes=62 << 20),
        name="pair_update",
    )(
        left, right, pair_features, output_weight, output_bias.reshape(1, C), norm_scale_gain.reshape(1, C),
        projection_weight, gate_offset_bias.reshape(1, C),
    )


def solution(mesh):
    placed = (P(("row", "col"), None), P("row", "col"), P("row", "col", None), P(), P(), P(), P(), P())
    return jax.shard_map(
        shards,
        mesh=mesh,
        in_specs=placed,
        out_specs=(P("row", "col", None), P("row", "col", None)),
        check_vma=False,
    )
```
